256 devices in a mesh: dp: 64 (over z, x, core), tensor: 4 (over y).
Axes of the slice: x: 4, y: 4, z: 8, core: 2. Of those that a mesh axis runs over, the one named last changes fastest.
Arguments:
- projections: bfloat16 [24576, 3, 3072], P('dp', None, 'tensor'), may hold values from -5.5 to 5.5
- routes: int32 [24576, 1], replicated, may hold values from 0 to 63; in each aligned block of 384 rows (0 to 383, 384 to 767, ...) at most 8 rows name the same one
- segments: int32 [64, 512], P('dp'), may hold values from 0 to 15, never falling along the last dimension, each value on 1 to 128 neighbouring positions
- out_weight: bfloat16 [3072, 6144], P('tensor'), may hold values from -0.109375 to 0.109375
Outputs:
- attention_out: bfloat16 [24576, 6144], P('dp', 'tensor')
The draws below stay inside these ranges and needn't reach their ends.
Inputs may be any that keep to these rules, and one draw needn't show every extreme that they name: `routes`: at most 8 of the 384 rows of one device name the same sequence, and in every draw the rows of some device name some sequence exactly 8 times. `segments`: in each row the image numbers never fall, each image covers 1 to 128 positions, and one image covers exactly 128.
All inputs are finite; a program needn't handle non-finite values.
Results may differ from the reference program's by a relative error of at most 0.009.
Values may be sent and summed in bfloat16 or wider, within the bound.
No kernel may reach another device: no remote copies, remote signals or barrier semaphores. Data moves between devices by JAX's collectives and lax.ppermute only.
A program may use at most 64 MiB of HBM per device.

```python
import math
import jax
import jax.numpy as jnp
import numpy as np
from jax import lax

D = 6144
HD = 128
HEADS = 24
OWN = 384
MAXP = 128
TOKENS = 24576
SLOT = 8
SEQ_POS = 512
SEGS = 16
N_DP = 64
N_TENSOR = 4


def draw_projections(key, part):
    full_shape = (TOKENS, 3, HEADS * HD)
    sub_keys = jax.random.split(key, 1)
    result = jnp.clip(jax.random.normal(sub_keys[0], full_shape, jnp.float32), -5.0, 5.0)
    return result.astype(jnp.bfloat16)


def level_of(rng, shape, cuts, smallest, high):
    factor_of, own = 1.0, jax.random.fold_in(rng, 6)
    for axis_at, parts in cuts:
        draws = jnp.exp(jax.random.uniform(jax.random.fold_in(own, axis_at), (parts,), jnp.float32, smallest / len(cuts), high / len(cuts)))
        factor_of = factor_of * jnp.repeat(draws, shape[axis_at] // parts).reshape([-1 if axis == axis_at else 1 for axis in range(len(shape))])
    return factor_of


def length_profile(amount, total, reach, lean):
    portions = [(1 << 20) // math.isqrt(rank ** lean) + 1 for rank in range(2, amount + 1)]
    surplus, counts = total - reach - (amount - 1), [1] * (amount - 1)
    while surplus > 0:
        candidates = [i for i in range(amount - 1) if counts[i] < reach]
        mass, left = sum([portions[i] for i in candidates]), surplus
        for i in candidates:
            extra = min(reach - counts[i], max(1, left * portions[i] // mass), surplus)
            counts[i] = counts[i] + extra
            surplus = surplus - extra
    return np.array([reach] + counts)


def uneven(stream_key, count, total, bound, skew):
    if count == 2:
        one = jax.random.randint(stream_key, (), max(1, total - bound), min(bound, total - 1) + 1)
        return jnp.stack([one, total - one])
    lengths = jnp.asarray(length_profile(count, total, bound, skew), jnp.int32)
    pairs = (count - 1) // 2
    giver, sink = lengths[1:1 + 2 * pairs:2], lengths[2:2 + 2 * pairs:2]
    slack = jnp.minimum(giver - 1, bound - sink)
    shifted = jax.random.randint(jax.random.fold_in(stream_key, 1), (pairs,), 0, 1 << 20) % (slack + 1)
    lengths = lengths.at[1:1 + 2 * pairs:2].set(giver - shifted).at[2:2 + 2 * pairs:2].set(sink + shifted)
    return lengths[jax.random.permutation(jax.random.fold_in(stream_key, 2), count)]


def assign_block(stream_key, own, number, rows, amount, top, reach, lean):
    ranking = jax.random.permutation(stream_key, amount)
    packed, ordinary = portions_of(amount, rows * top, reach, lean, True), portions_of(amount, rows * top, reach, lean, False)
    places = jnp.arange(amount)

    def named(sizes, offset_by):
        used = int((sizes > 0).sum())
        fixed = max(1, used // 4)
        shifted = fixed + (places - fixed + offset_by * (used - fixed)) % max(1, amount - fixed)
        return jnp.zeros((amount,), jnp.int32).at[ranking[jnp.where(places < fixed, places, shifted)]].set(jnp.asarray(sizes, jnp.int32))

    sizes = jnp.where(number % 4 == 0, named(packed, number // 4), named(ordinary, number - number // 4 - 1))
    mixed = jax.random.permutation(jax.random.fold_in(own, 3), amount)
    giver, sink = mixed[0:amount // 2 * 2:2], mixed[1:amount // 2 * 2:2]
    margin = jnp.minimum(sizes[giver] - 1, reach - sizes[sink]) // 2
    margin = jnp.where((giver == ranking[0]) | (sink == ranking[0]) | (sizes[sink] == 0), 0, jnp.maximum(margin, 0))
    shifted = jax.random.randint(jax.random.fold_in(own, 4), (amount // 2,), 0, 1 << 20) % (margin + 1)
    sizes = sizes.at[giver].add(-shifted).at[sink].add(shifted)
    members = jnp.searchsorted(jnp.cumsum(sizes), jnp.arange(rows * top), side="right").astype(jnp.int32)
    listing = members.reshape(top, rows).T
    listing = listing[jax.random.permutation(jax.random.fold_in(own, 1), rows)]
    offset_by = jax.random.randint(jax.random.fold_in(own, 2), (rows, 1), 0, top)
    return jnp.take_along_axis(listing, (jnp.arange(top)[None, :] + offset_by) % top, axis=1)


def portions_of(amount, total, limit, skew, full):
    weights = [(1 << 20) // math.isqrt(rank ** skew) + 1 for rank in range(1, amount + 1)]
    largest = limit if full else min(limit, max(-(-total // amount), total * weights[0] // sum(weights)))
    least = 1 if total - largest >= amount - 1 else 0
    counts, surplus = [largest] + [least] * (amount - 1), total - largest - least * (amount - 1)
    while surplus > 0:
        movable = [i for i in range(1, amount) if counts[i] < largest] or [i for i in range(1, amount) if counts[i] < limit]
        mass, remaining = sum([weights[i] for i in movable]), surplus
        for i in movable:
            addition = min(limit - counts[i], max(1, remaining * weights[i] // mass), surplus)
            counts[i] = counts[i] + addition
            surplus = surplus - addition
    return np.array(counts)


def centred(rng, dims, scale, limit, shards=(), held_as=jnp.bfloat16):
    values = jax.random.normal(rng, dims, jnp.float32) * scale
    if len(shards) > 0:
        values = level_of(rng, dims, shards, -0.22, 0.18) * values
    return jnp.clip(values, min=-limit, max=limit).astype(held_as)


def setup_inputs(seed: int = 0) -> dict:
    streams_of = jax.random.split(jax.random.key(seed), 5)
    projections = draw_projections(jax.random.fold_in(streams_of[4], 71), 0)
    routes_keys = jax.random.split(jax.random.fold_in(streams_of[1], 1), TOKENS // OWN)
    routes_turns = jax.random.permutation(jax.random.fold_in(streams_of[1], 3), TOKENS // OWN)
    routes = jax.vmap(lambda own, number: assign_block(jax.random.fold_in(streams_of[1], 2), own, number, OWN, N_DP, 1, SLOT, 2))(routes_keys, routes_turns).reshape((TOKENS, 1))
    segments = jax.vmap(lambda own: jnp.searchsorted(jnp.cumsum(uneven(own, SEGS, SEQ_POS, MAXP, 2)), jnp.arange(SEQ_POS), side="right"))(jax.random.split(streams_of[2], N_DP)).reshape((N_DP, SEQ_POS)).astype(jnp.int32)
    out_weight = centred(streams_of[3], (HEADS * HD, D), (HEADS * HD) ** -0.5, 0.109375, ((0, 4),))
    return {"projections": projections, "routes": routes, "segments": segments, "out_weight": out_weight}


def attend_sequence(block_pair):
    packed_rows, group_ids = block_pair
    queries = packed_rows[:, 0].astype(jnp.float32)
    keys_in = packed_rows[:, 1].astype(jnp.float32)
    values_in = packed_rows[:, 2].astype(jnp.float32)
    allowed = group_ids[:, None] == group_ids[None, :]
    scores = jnp.einsum('qhd,khd->hqk', queries, keys_in) * (1.0 / math.sqrt(HD))
    scores = jnp.where(allowed[None], scores, -jnp.inf)
    highest = lax.optimization_barrier(jnp.max(scores, axis=2, keepdims=True))
    raised = jnp.exp(scores - highest)
    weights = (raised / lax.optimization_barrier(jnp.sum(raised, axis=2, keepdims=True))).astype(jnp.bfloat16)
    weights = lax.optimization_barrier(weights)
    attended = jnp.einsum('hqk,khd->qhd', weights.astype(jnp.float32), values_in)
    return attended.astype(jnp.bfloat16)

def reference(projections, routes, segments, out_weight):
    targets = routes[:, 0]
    one_hot = (targets[:, None] == jnp.arange(N_DP, dtype=jnp.int32)[None, :]).astype(jnp.int32)
    position = lax.optimization_barrier(jnp.sum((jnp.cumsum(one_hot, axis=0) - one_hot) * one_hot, axis=1)).astype(jnp.int32)
    flat_slot = (targets * SEQ_POS + position).astype(jnp.int32)
    source_row = jnp.zeros((N_DP * SEQ_POS,), jnp.int32).at[flat_slot].set(jnp.arange(TOKENS, dtype=jnp.int32))
    filled = jnp.zeros((N_DP * SEQ_POS,), jnp.int32).at[flat_slot].set(1).reshape(N_DP, SEQ_POS)
    gathered = projections[source_row].reshape(N_DP, SEQ_POS, 3, HEADS, HD)
    unique_ids = -1 - jnp.arange(SEQ_POS, dtype=jnp.int32)
    group_ids = jnp.where(filled > 0, segments, unique_ids[None, :])
    per_sequence = lax.map(attend_sequence, (gathered, group_ids))
    attended = per_sequence.reshape(N_DP * SEQ_POS, HEADS * HD)[flat_slot]
    columns = HEADS * HD // N_TENSOR
    total = jnp.zeros((TOKENS, D), jnp.float32)
    for group in range(N_TENSOR):
        piece = jnp.dot(attended[:, group * columns:(group + 1) * columns], out_weight[group * columns:(group + 1) * columns], preferred_element_type=jnp.float32).astype(jnp.bfloat16)
        piece = lax.optimization_barrier(piece)
        total = total + piece.astype(jnp.float32)
    return total.astype(jnp.bfloat16)
```

```python
import functools
import math

import jax
import jax.numpy as jnp
from jax import lax
from jax.experimental import pallas as pl
from jax.experimental.pallas import tpu as pltpu
from jax.sharding import PartitionSpec as P


HD = 128
VMEM = pltpu.MemorySpace.VMEM
HBM = pltpu.MemorySpace.HBM


def pack_kernel(capacity, rows_ref, data_ref, slot_ref, out_ref, held, built, in_sem, out_sem):
    own_rows = rows_ref.shape[1]
    positions = out_ref.shape[0]
    kinds, _, width = data_ref.shape
    senders = positions // capacity
    arriving = [
        pltpu.make_async_copy(data_ref.at[kind], held.at[kind], in_sem.at[kind])
        for kind in range(kinds)
    ]
    for copy in arriving:
        copy.start()
    routes = rows_ref[...]
    chosen = lax.broadcasted_iota(jnp.int32, (senders, own_rows), 0) == routes
    earlier = lax.broadcasted_iota(jnp.int32, (own_rows, own_rows), 0) < lax.broadcasted_iota(
        jnp.int32, (own_rows, own_rows), 1
    )
    counts = jnp.dot(
        chosen.astype(jnp.bfloat16),
        earlier.astype(jnp.bfloat16),
        preferred_element_type=jnp.float32,
    )
    ranking = jnp.sum(jnp.where(chosen, counts, 0.0), axis=0, keepdims=True).astype(jnp.int32)
    slots = routes * capacity + ranking
    slot_ref[...] = slots
    place = (lax.broadcasted_iota(jnp.int32, (positions, own_rows), 0) == slots).astype(
        jnp.bfloat16
    )
    leaving = []
    for kind in range(kinds):
        columns = slice(kind * width, (kind + 1) * width)
        arriving[kind].wait()
        built[:, columns] = jnp.dot(
            place, held[kind], preferred_element_type=jnp.float32
        ).astype(jnp.bfloat16)
        leaving.append(
            pltpu.make_async_copy(built.at[:, columns], out_ref.at[:, columns], out_sem.at[kind])
        )
        leaving[kind].start()
    for copy in leaving:
        copy.wait()


def pack(my_routes, by_kind, positions, capacity):
    kinds, own_rows, width = by_kind.shape
    return pl.pallas_call(
        functools.partial(pack_kernel, capacity),
        out_shape=(
            jax.ShapeDtypeStruct((1, own_rows), jnp.int32),
            jax.ShapeDtypeStruct((positions, kinds * width), jnp.bfloat16),
        ),
        in_specs=[pl.BlockSpec(memory_space=VMEM), pl.BlockSpec(memory_space=HBM)],
        out_specs=(pl.BlockSpec(memory_space=VMEM), pl.BlockSpec(memory_space=HBM)),
        scratch_shapes=[
            pltpu.VMEM(by_kind.shape, jnp.bfloat16),
            pltpu.VMEM((positions, kinds * width), jnp.bfloat16),
            pltpu.SemaphoreType.DMA((kinds,)),
            pltpu.SemaphoreType.DMA((kinds,)),
        ],
        name="pack_rows",
    )(my_routes.reshape(1, own_rows), by_kind)


def attend_kernel(heads, group_col_ref, group_row_ref, data_ref, out_ref):
    width = heads * HD
    allowed = group_col_ref[...] == group_row_ref[...]
    scale = 1.0 / math.sqrt(HD)
    for head in range(heads):
        low, high = head * HD, (head + 1) * HD
        queries = data_ref[:, low:high]
        keys_in = data_ref[:, width + low : width + high]
        values_in = data_ref[:, 2 * width + low : 2 * width + high]
        scores = lax.dot_general(
            queries, keys_in, (((1,), (1,)), ((), ())), preferred_element_type=jnp.float32
        )
        scores = jnp.where(allowed, scores * scale, -jnp.inf)
        highest = jnp.max(scores, axis=1, keepdims=True)
        raised = jnp.exp(scores - highest)
        total = jnp.sum(raised, axis=1, keepdims=True)
        mixed = jnp.dot(
            raised.astype(jnp.bfloat16), values_in, preferred_element_type=jnp.float32
        )
        out_ref[:, low:high] = (mixed / total).astype(jnp.bfloat16)


def attend(group_ids, arrived, heads):
    positions = arrived.shape[0]
    return pl.pallas_call(
        functools.partial(attend_kernel, heads),
        out_shape=jax.ShapeDtypeStruct((positions, heads * HD), jnp.bfloat16),
        in_specs=[pl.BlockSpec(memory_space=VMEM)] * 3,
        out_specs=pl.BlockSpec(memory_space=VMEM),
        compiler_params=pltpu.CompilerParams(vmem_limit_bytes=20 * 2**20),
        name="attend_rows",
    )(group_ids.reshape(positions, 1), group_ids.reshape(1, positions), arrived)


def local(projections, routes, segments, out_weight):
    senders = lax.axis_size("dp")
    groups = lax.axis_size("tensor")
    myself = lax.axis_index("dp")
    my_group = lax.axis_index("tensor")
    own_rows = projections.shape[0]
    column_count = projections.shape[2]
    heads_here = column_count // HD
    positions = segments.shape[1]
    capacity = positions // senders
    out_columns = out_weight.shape[1] // groups
    targets = routes[:, 0]
    my_routes = lax.dynamic_slice_in_dim(targets, myself * own_rows, own_rows)
    slots, outgoing = pack(my_routes, jnp.transpose(projections, (1, 0, 2)), positions, capacity)
    arrived = lax.all_to_all(
        outgoing.reshape(senders, capacity, 3 * column_count),
        "dp",
        split_axis=0,
        concat_axis=0,
        tiled=True,
    ).reshape(positions, 3 * column_count)

    arrivals = jnp.sum((targets.reshape(senders, own_rows) == myself).astype(jnp.int32), axis=1)
    earlier = jnp.cumsum(arrivals) - arrivals
    within = jnp.arange(capacity, dtype=jnp.int32)
    placed = earlier[:, None] + within[None, :]
    filled = within[None, :] < arrivals[:, None]
    flat_index = jnp.arange(positions, dtype=jnp.int32).reshape(senders, capacity)
    looked_up = segments[0][jnp.minimum(placed, positions - 1)]
    group_ids = jnp.where(filled, looked_up, -1 - flat_index).reshape(positions)
    restore = (
        slots.reshape(own_rows, 1) == jnp.arange(positions, dtype=jnp.int32)[None, :]
    ).astype(jnp.bfloat16)

    def shifted(value, step):
        return lax.ppermute(
            value, "tensor", [(here, (here + step) % groups) for here in range(groups)]
        )

    def weight_columns(step):
        at = lax.rem(my_group + step, groups) * out_columns
        return lax.dynamic_slice_in_dim(out_weight, at, out_columns, axis=1)

    weights = [weight_columns(0)]
    for step in range(1, groups):
        weights.append(shifted(weight_columns(step), step))

    attended = attend(group_ids, arrived, heads_here)
    returned = lax.all_to_all(
        attended.reshape(senders, capacity, column_count),
        "dp",
        split_axis=0,
        concat_axis=0,
        tiled=True,
    ).reshape(positions, column_count)
    mine = jnp.dot(restore, returned, preferred_element_type=jnp.float32).astype(jnp.bfloat16)
    pieces = [mine]
    for step in range(1, groups):
        pieces.append(shifted(mine, step))
    total = jnp.dot(pieces[0], weights[0], preferred_element_type=jnp.float32)
    for step in (1, 3, 2):
        total = total + jnp.dot(pieces[step], weights[step], preferred_element_type=jnp.float32)
    return total.astype(jnp.bfloat16)


def solution(mesh):
    in_specs = (P("dp", None, "tensor"), P(), P("dp", None), P("tensor", None))
    out_specs = P("dp", "tensor")
    return jax.shard_map(local, mesh=mesh, in_specs=in_specs, out_specs=out_specs, check_vma=False)
```

```python
import functools
import math

import jax
import jax.numpy as jnp
from jax import lax
from jax.experimental import pallas as pl
from jax.experimental.pallas import tpu as pltpu
from jax.sharding import PartitionSpec as P


HD = 128
VMEM = pltpu.MemorySpace.VMEM
HBM = pltpu.MemorySpace.HBM


def pack_kernel(
    capacity, routes_ref, data_ref, slot_ref, out_ref, named, held, built, in_sem, out_sem
):
    own_rows = named.shape[1]
    positions = out_ref.shape[0]
    kinds, _, width = data_ref.shape
    senders = positions // capacity
    arriving = [
        pltpu.make_async_copy(data_ref.at[kind], held.at[kind], in_sem.at[kind])
        for kind in range(kinds)
    ]
    own_at = pl.multiple_of(lax.axis_index("dp") * own_rows, own_rows)
    naming = pltpu.make_async_copy(
        routes_ref.at[:, pl.ds(own_at, own_rows)], named, in_sem.at[kinds]
    )
    naming.start()
    for copy in arriving:
        copy.start()
    naming.wait()
    routes = named[...]
    chosen = lax.broadcasted_iota(jnp.int32, (senders, own_rows), 0) == routes
    earlier = lax.broadcasted_iota(jnp.int32, (own_rows, own_rows), 0) < lax.broadcasted_iota(
        jnp.int32, (own_rows, own_rows), 1
    )
    counts = jnp.dot(
        chosen.astype(jnp.bfloat16),
        earlier.astype(jnp.bfloat16),
        preferred_element_type=jnp.float32,
    )
    ranking = jnp.sum(jnp.where(chosen, counts, 0.0), axis=0, keepdims=True).astype(jnp.int32)
    slots = routes * capacity + ranking
    slot_ref[...] = slots
    place = (lax.broadcasted_iota(jnp.int32, (positions, own_rows), 0) == slots).astype(
        jnp.bfloat16
    )
    leaving = []
    for kind in range(kinds):
        columns = slice(kind * width, (kind + 1) * width)
        arriving[kind].wait()
        built[:, columns] = jnp.dot(
            place, held[kind], preferred_element_type=jnp.float32
        ).astype(jnp.bfloat16)
        leaving.append(
            pltpu.make_async_copy(built.at[:, columns], out_ref.at[:, columns], out_sem.at[kind])
        )
        leaving[kind].start()
    for copy in leaving:
        copy.wait()


def pack(routes, by_kind, positions, capacity):
    kinds, own_rows, width = by_kind.shape
    return pl.pallas_call(
        functools.partial(pack_kernel, capacity),
        out_shape=(
            jax.ShapeDtypeStruct((1, own_rows), jnp.int32),
            jax.ShapeDtypeStruct((positions, kinds * width), jnp.bfloat16),
        ),
        in_specs=[pl.BlockSpec(memory_space=HBM)] * 2,
        out_specs=(pl.BlockSpec(memory_space=VMEM), pl.BlockSpec(memory_space=HBM)),
        scratch_shapes=[
            pltpu.VMEM((1, own_rows), jnp.int32),
            pltpu.VMEM(by_kind.shape, jnp.bfloat16),
            pltpu.VMEM((positions, kinds * width), jnp.bfloat16),
            pltpu.SemaphoreType.DMA((kinds + 1,)),
            pltpu.SemaphoreType.DMA((kinds,)),
        ],
        name="pack_rows",
    )(routes, by_kind)


def attend_kernel(
    heads, group_col_ref, group_row_ref, data_ref, out_ref, held, built, in_sem, out_sem
):
    width = heads * HD
    arriving, leaving = [], []
    for head in range(heads):
        parts = []
        for kind in range(3):
            low = kind * width + head * HD
            columns = slice(low, low + HD)
            parts.append(
                pltpu.make_async_copy(
                    data_ref.at[:, columns], held.at[:, columns], in_sem.at[3 * head + kind]
                )
            )
            parts[kind].start()
        arriving.append(parts)
    allowed = group_col_ref[...] == group_row_ref[...]
    scale = 1.0 / math.sqrt(HD)
    for head in range(heads):
        low, high = head * HD, (head + 1) * HD
        for copy in arriving[head]:
            copy.wait()
        queries = held[:, low:high]
        keys_in = held[:, width + low : width + high]
        values_in = held[:, 2 * width + low : 2 * width + high]
        scores = lax.dot_general(
            queries, keys_in, (((1,), (1,)), ((), ())), preferred_element_type=jnp.float32
        )
        scores = jnp.where(allowed, scores * scale, -jnp.inf)
        highest = jnp.max(scores, axis=1, keepdims=True)
        raised = jnp.exp(scores - highest)
        total = jnp.sum(raised, axis=1, keepdims=True)
        mixed = jnp.dot(
            raised.astype(jnp.bfloat16), values_in, preferred_element_type=jnp.float32
        )
        built[:, low:high] = (mixed / total).astype(jnp.bfloat16)
        leaving.append(
            pltpu.make_async_copy(
                built.at[:, low:high], out_ref.at[:, low:high], out_sem.at[head]
            )
        )
        leaving[head].start()
    for copy in leaving:
        copy.wait()


def attend(group_ids, arrived, heads):
    positions = arrived.shape[0]
    shape = (positions, heads * HD)
    return pl.pallas_call(
        functools.partial(attend_kernel, heads),
        out_shape=jax.ShapeDtypeStruct(shape, jnp.bfloat16),
        in_specs=[pl.BlockSpec(memory_space=VMEM)] * 2 + [pl.BlockSpec(memory_space=HBM)],
        out_specs=pl.BlockSpec(memory_space=HBM),
        scratch_shapes=[
            pltpu.VMEM(arrived.shape, jnp.bfloat16),
            pltpu.VMEM(shape, jnp.bfloat16),
            pltpu.SemaphoreType.DMA((3 * heads,)),
            pltpu.SemaphoreType.DMA((heads,)),
        ],
        name="attend_rows",
    )(group_ids.reshape(positions, 1), group_ids.reshape(1, positions), arrived)


def restore_kernel(at_ref, place_ref, data_ref, first_ref, second_ref):
    half = first_ref.shape[1]
    for at, out_ref in ((at_ref[0], first_ref), (half - at_ref[0], second_ref)):
        columns = data_ref[:, pl.ds(pl.multiple_of(at, half), half)]
        out_ref[...] = jnp.dot(
            place_ref[...], columns, preferred_element_type=jnp.float32
        ).astype(jnp.bfloat16)


def restored(first_at, place, data):
    shape = jax.ShapeDtypeStruct((place.shape[0], data.shape[1] // 2), jnp.bfloat16)
    return pl.pallas_call(
        restore_kernel,
        out_shape=(shape, shape),
        in_specs=[pl.BlockSpec(memory_space=pltpu.MemorySpace.SMEM)]
        + [pl.BlockSpec(memory_space=VMEM)] * 2,
        out_specs=(pl.BlockSpec(memory_space=VMEM),) * 2,
        compiler_params=pltpu.CompilerParams(vmem_limit_bytes=20 * 2**20),
        name="restore_rows",
    )(first_at.reshape(1), place, data)


def mix_kernel(count, has_total, *refs):
    rows, weights = refs[:count], refs[count : 2 * count]
    out_ref = refs[2 * count + has_total]
    width = out_ref.shape[1]
    step = 512
    staged = refs[2 * count + has_total + 1 :]
    copies = []
    for at, low in enumerate(range(0, width, step)):
        columns = slice(low, low + step)
        total = refs[2 * count][:, columns] if has_total else None
        for row, weight in zip(rows, weights):
            term = jnp.dot(row[...], weight[:, columns], preferred_element_type=jnp.float32)
            total = term if total is None else total + term
        if staged:
            staged[0][:, columns] = total.astype(staged[0].dtype)
            copies.append(
                pltpu.make_async_copy(
                    staged[0].at[:, columns], out_ref.at[:, columns], staged[1].at[at]
                )
            )
            copies[at].start()
        else:
            out_ref[:, columns] = total
    for copy in copies:
        copy.wait()


def mix(rows, weights, total=None, last=False):
    shape = (rows[0].shape[0], weights[0].shape[1])
    given = [*rows, *weights] + ([] if total is None else [total])
    dtype = jnp.bfloat16 if last else jnp.float32
    return pl.pallas_call(
        functools.partial(mix_kernel, len(rows), total is not None),
        out_shape=jax.ShapeDtypeStruct(shape, dtype),
        in_specs=[pl.BlockSpec(memory_space=VMEM)] * len(given),
        out_specs=pl.BlockSpec(memory_space=HBM if last else VMEM),
        scratch_shapes=(
            [pltpu.VMEM(shape, dtype), pltpu.SemaphoreType.DMA((shape[1] // 512,))] if last else []
        ),
        compiler_params=pltpu.CompilerParams(vmem_limit_bytes=20 * 2**20),
        name="mix_last" if last else "mix_some",
    )(*given)


def local(projections, routes, segments, out_weight):
    senders = lax.axis_size("dp")
    groups = lax.axis_size("tensor")
    myself = lax.axis_index("dp")
    my_group = lax.axis_index("tensor")
    own_rows = projections.shape[0]
    column_count = projections.shape[2]
    heads_here = column_count // HD
    positions = segments.shape[1]
    capacity = positions // senders
    out_columns = out_weight.shape[1] // groups
    half = column_count // 2
    first_at = (myself % 2) * half
    second_at = half - first_at
    targets = routes[:, 0]
    slots, outgoing = pack(
        targets.reshape(1, senders * own_rows),
        jnp.transpose(projections, (1, 0, 2)),
        positions,
        capacity,
    )
    arrived = lax.all_to_all(
        outgoing.reshape(senders, capacity, 3 * column_count),
        "dp",
        split_axis=0,
        concat_axis=0,
        tiled=True,
    ).reshape(positions, 3 * column_count)

    arrivals = jnp.sum((targets.reshape(senders, own_rows) == myself).astype(jnp.int32), axis=1)
    earlier = jnp.cumsum(arrivals) - arrivals
    within = jnp.arange(capacity, dtype=jnp.int32)
    placed = earlier[:, None] + within[None, :]
    filled = within[None, :] < arrivals[:, None]
    flat_index = jnp.arange(positions, dtype=jnp.int32).reshape(senders, capacity)
    looked_up = segments[0][jnp.minimum(placed, positions - 1)]
    group_ids = jnp.where(filled, looked_up, -1 - flat_index).reshape(positions)
    restore = (
        slots.reshape(own_rows, 1) == jnp.arange(positions, dtype=jnp.int32)[None, :]
    ).astype(jnp.bfloat16)

    def shifted(value, step):
        return lax.ppermute(
            value, "tensor", [(here, (here + step) % groups) for here in range(groups)]
        )

    def traded(value):
        return lax.ppermute(value, "dp", [(here, here ^ 1) for here in range(senders)])

    def weight_block(row_at, step):
        column_at = lax.rem(my_group + step, groups) * out_columns
        return lax.dynamic_slice(out_weight, (row_at, column_at), (half, out_columns))

    weights = {}
    for step in (1, 3, 2):
        weights[step] = (shifted(weight_block(first_at, step), step),)

    attended = attend(group_ids, arrived, heads_here)
    returned = lax.all_to_all(
        attended.reshape(senders, capacity, column_count),
        "dp",
        split_axis=0,
        concat_axis=0,
        tiled=True,
    ).reshape(positions, column_count)
    for step in (1, 3, 2):
        weights[step] += (traded(weights[step][0]),)

    first, second = restored(first_at, restore, returned)
    left_first = shifted(first, 1)
    right_second = shifted(second, -1)
    left_second = shifted(second, 1)
    right_first = shifted(first, -1)
    total = mix((first, second), (weight_block(first_at, 0), weight_block(second_at, 0)))
    far_first = shifted(left_first, 1)
    far_second = shifted(right_second, -1)
    total = mix(
        (left_first, left_second, right_first, right_second), weights[1] + weights[3], total
    )
    return mix((far_first, far_second), weights[2], total, last=True)


def solution(mesh):
    in_specs = (P("dp", None, "tensor"), P(), P("dp", None), P("tensor", None))
    out_specs = P("dp", "tensor")
    return jax.shard_map(local, mesh=mesh, in_specs=in_specs, out_specs=out_specs, check_vma=False)
```
